32 devices in a mesh: row: 8 (over y, x, core), col: 4 (over z).
Axes of the slice: x: 2, y: 2, z: 4, core: 2. Of those that a mesh axis runs over, the one named last changes fastest.
Arguments:
- covariance: float32 [8192, 8192], P('row', 'col'), may hold values from -8 to 8, as said below
- model_noise: float32 [8192], replicated, may hold values from 0.2 to 1
- east_wind: float32 [2, 64, 128], replicated, may hold values from -0.45 to 0.45
- north_wind: float32 [2, 64, 128], replicated, may hold values from -0.45 to 0.45
Outputs:
- forecast: float32 [8192, 8192], P('row', 'col')
The draws below stay inside these ranges and needn't reach their ends.
Inputs may be any that keep to these rules, and one draw needn't show every extreme that they name: `covariance`: symmetric.
All inputs are finite; a program needn't handle non-finite values.
Results may differ from the reference program's by a relative error of at most 0.00002.
Values sent between devices are 32-bit elements; how exact they have to be, the bound alone decides.
A program may use at most 128 MiB of HBM per device.

```python
import math
import jax
import jax.numpy as jnp
from jax import lax

NLAT = 64
NLON = 128
CYCLES = 2
M = 8192


def draw_covariance(key, part):
    base = jax.random.fold_in(key, 7)
    sample = jnp.clip(jax.random.normal(base, (M, M), jnp.float32), -6.0, 6.0)
    return 0.5 * (sample + sample.T)


def setup_inputs(seed: int = 0) -> dict:
    seeds = jax.random.split(jax.random.key(seed), 5)
    return {
        "covariance": draw_covariance(jax.random.fold_in(seeds[4], 71), 0),
        "model_noise": jnp.clip(jnp.exp(jax.random.uniform(seeds[1], (M,), jnp.float32, math.log(0.2), math.log(1.0))), 0.2, 1.0),
        "east_wind": jnp.clip(jax.random.uniform(seeds[2], (CYCLES, NLAT, NLON), jnp.float32, -0.45, 0.45), -0.45, 0.45),
        "north_wind": jnp.clip(jax.random.uniform(seeds[3], (CYCLES, NLAT, NLON), jnp.float32, -0.45, 0.45), -0.45, 0.45),
    }


def tendency(padded, east_now, faces_now, lat_axis, expand):
    lon_axis = lat_axis + 1
    lines = padded.shape[lat_axis] - 2
    middle = lax.slice_in_dim(padded, 1, lines + 1, axis=lat_axis)
    eastward = jnp.roll(middle, -1, axis=lon_axis)
    courant = expand(east_now)
    flux_east = jnp.maximum(courant, 0.0) * middle + jnp.minimum(courant, 0.0) * eastward
    flux_west = jnp.roll(flux_east, 1, axis=lon_axis)
    below = lax.slice_in_dim(padded, 0, lines + 1, axis=lat_axis)
    above = lax.slice_in_dim(padded, 1, lines + 2, axis=lat_axis)
    northern = expand(faces_now)
    flux_north = jnp.maximum(northern, 0.0) * below + jnp.minimum(northern, 0.0) * above
    south_in = lax.slice_in_dim(flux_north, 0, lines, axis=lat_axis)
    north_out = lax.slice_in_dim(flux_north, 1, lines + 1, axis=lat_axis)
    return (flux_west - flux_east) + (south_in - north_out)


def rows_form(values):
    return values[:, :, None]


def cols_form(values):
    return values[None, :, :]


def pad_lines(field, lat_axis):
    widths = [(0, 0)] * field.ndim
    widths[lat_axis] = (1, 1)
    return jnp.pad(field, widths)


def heun_full(field, east_now, faces_now, lat_axis, expand):
    section_one = field + tendency(pad_lines(field, lat_axis), east_now, faces_now, lat_axis, expand)
    tend_two = tendency(pad_lines(section_one, lat_axis), east_now, faces_now, lat_axis, expand)
    return 0.5 * ((field + section_one) + tend_two)


def reference(covariance, model_noise, east_wind, north_wind):
    width = M // 8
    state = covariance
    positions = jnp.arange(M, dtype=jnp.int32)
    for cycle_index in range(CYCLES):
        east_now = east_wind[cycle_index]
        faces_now = jnp.concatenate([jnp.zeros((1, NLON), north_wind.dtype), north_wind[cycle_index]], axis=0)

        def column_block(index):
            piece = lax.dynamic_slice_in_dim(state, index * width, width, 1)
            moved = heun_full(piece.reshape(NLAT, NLON, width), east_now, faces_now, 0, rows_form)
            return moved.reshape(M, width)

        blocks = lax.map(column_block, jnp.arange(8, dtype=jnp.int32))
        half = jnp.transpose(blocks, (1, 0, 2)).reshape(M, M)

        def row_block(index):
            piece = lax.dynamic_slice_in_dim(half, index * width, width, 0)
            moved = heun_full(piece.reshape(width, NLAT, NLON), east_now, faces_now, 1, cols_form)
            return moved.reshape(width, M)

        state = lax.map(row_block, jnp.arange(8, dtype=jnp.int32)).reshape(M, M)
        state = state.at[positions, positions].add(model_noise)
    return state
```

```python
import jax
import jax.numpy as jnp
from jax import lax
from jax.experimental import pallas as pl
from jax.experimental.pallas import tpu as pltpu
from jax.sharding import PartitionSpec as P

NLON = 128
CYCLES = 2
HALO = 2 * CYCLES


def coefficients(east, north):
    west = jnp.roll(east, 1, axis=-1)
    south = jnp.pad(north[:, :-1], ((0, 0), (1, 0), (0, 0)))
    up, down = (lambda v: jnp.maximum(v, 0.0)), (lambda v: jnp.minimum(v, 0.0))
    centre = 1.0 + ((down(west) - up(east)) + (down(south) - up(north)))
    to_north = -down(north)
    lines = north.shape[1]
    inside = (jnp.arange(lines) < lines - 1)[None, :, None]
    to_north = jnp.where(inside, to_north, 0.0)
    return jnp.stack([centre, -down(east), up(west), to_north, up(south)], axis=1)


def lines_of(coef, first, amount):
    padded = jnp.pad(coef, ((0, 0), (0, 0), (2 * HALO, 2 * HALO), (0, 0)))
    return lax.dynamic_slice_in_dim(padded, first + 2 * HALO, amount, 2)


def stencil(centre, east, west, north, south, c):
    return (c[0] * centre + (c[1] * east + c[2] * west)) + (c[3] * north + c[4] * south)


def row_kernel(lines, before_ref, mid_ref, after_ref, coef_ref, out_ref, one, two, three):
    total = lines + 2 * HALO
    width = 128

    def tile(j, carry):
        cols = pl.ds(pl.multiple_of(j * width, width), width)

        def source(l):
            if l < HALO:
                return before_ref[l * NLON:(l + 1) * NLON, cols]
            if l < HALO + lines:
                return mid_ref[(l - HALO) * NLON:(l - HALO + 1) * NLON, cols]
            l = l - HALO - lines
            return after_ref[l * NLON:(l + 1) * NLON, cols]

        def kept(ref):
            return lambda l: ref[l * NLON:(l + 1) * NLON, :]

        def step(read, l, cycle):
            c = [coef_ref[cycle * 5 + i, l * NLON:(l + 1) * NLON, :] for i in range(5)]
            g = read(l)
            return stencil(
                g, pltpu.roll(g, NLON - 1, 0), pltpu.roll(g, 1, 0), read(l + 1), read(l - 1), c
            )

        for l in range(1, total - 1):
            one[l * NLON:(l + 1) * NLON, :] = step(source, l, 0)
        for l in range(2, total - 2):
            two[l * NLON:(l + 1) * NLON, :] = 0.5 * (source(l) + step(kept(one), l, 0))
        for l in range(3, total - 3):
            three[l * NLON:(l + 1) * NLON, :] = step(kept(two), l, 1)
        for l in range(4, total - 4):
            value = 0.5 * (kept(two)(l) + step(kept(three), l, 1))
            out_ref[(l - HALO) * NLON:(l - HALO + 1) * NLON, cols] = value
        return carry

    lax.fori_loop(0, out_ref.shape[1] // width, tile, 0)


def row_sections(before, block, after, coef, rows, columns, chunk, tile):
    lines = rows // NLON
    total = rows + 2 * HALO * NLON
    per = columns // tile
    return pl.pallas_call(
        lambda *refs: row_kernel(lines, *refs),
        out_shape=jax.ShapeDtypeStruct((rows, columns), jnp.float32),
        grid=(per,),
        in_specs=[
            pl.BlockSpec((HALO * NLON, tile), lambda i: (0, i)),
            pl.BlockSpec((rows, tile), lambda i: (0, chunk * per + i)),
            pl.BlockSpec((HALO * NLON, tile), lambda i: (0, i)),
            pl.BlockSpec((5 * CYCLES, total, 128), lambda i: (0, 0, 0), pipeline_mode=pl.Buffered(1)),
        ],
        out_specs=pl.BlockSpec((rows, tile), lambda i: (0, i)),
        scratch_shapes=[pltpu.VMEM((total, 128), jnp.float32)] * 3,
        compiler_params=pltpu.CompilerParams(vmem_limit_bytes=40 << 20),
        cost_estimate=pl.CostEstimate(
            flops=60 * rows * columns, transcendentals=0, bytes_accessed=12 * rows * columns + (10 << 20)
        ),
        name="row_sections",
    )(before, block, after, coef)


def col_kernel(lines, chunks, sub, place_ref, *refs):
    before_ref, mids, after_ref = refs[0], refs[1:1 + chunks], refs[1 + chunks]
    coef_ref, noise_ref, out_ref, one, two, three = refs[2 + chunks:]
    total = lines + 2 * HALO
    each = lines // chunks
    row_line = place_ref[0] + pl.program_id(0) * out_ref.shape[0] // NLON
    shift = row_line - place_ref[1]

    def lane(l):
        return slice(l * NLON, (l + 1) * NLON)

    def part(j, carry):
        rows = pl.ds(pl.multiple_of(j * sub, sub), sub)

        def source(l):
            if l < HALO:
                return before_ref[rows, lane(l)]
            if l < HALO + lines:
                m, k = divmod(l - HALO, each)
                return mids[m][rows, lane(k)]
            return after_ref[rows, lane(l - HALO - lines)]

        def kept(ref):
            return lambda l: ref[:, lane(l)]

        def step(read, l, cycle):
            c = [
                jnp.broadcast_to(coef_ref[cycle * 5 + i:cycle * 5 + i + 1, lane(l)], (sub, NLON))
                for i in range(5)
            ]
            g = read(l)
            return stencil(
                g, pltpu.roll(g, NLON - 1, 1), pltpu.roll(g, 1, 1), read(l + 1), read(l - 1), c
            )

        for l in range(1, total - 1):
            one[:, lane(l)] = step(source, l, 0)
        for l in range(2, total - 2):
            two[:, lane(l)] = 0.5 * (source(l) + step(kept(one), l, 0))
        for d in range(5):
            at = shift + (d - 2 + HALO)

            @pl.when((at >= 2) & (at < total - 2))
            def _():
                cols = pl.ds(pl.multiple_of(at * NLON, NLON), NLON)
                two[:, cols] = two[:, cols] + noise_ref[rows, lane(d)]

        for l in range(3, total - 3):
            three[:, lane(l)] = step(kept(two), l, 1)
        for l in range(4, total - 4):
            out_ref[rows, lane(l - HALO)] = 0.5 * (kept(two)(l) + step(kept(three), l, 1))

        @pl.when((shift >= 0) & (shift < lines))
        def _():
            cols = pl.ds(pl.multiple_of(shift * NLON, NLON), NLON)
            out_ref[rows, cols] = out_ref[rows, cols] + noise_ref[rows, lane(5)]

        return carry

    lax.fori_loop(0, out_ref.shape[0] // sub, part, 0)


def col_sections(place, before, mids, after, coef, noise, rows, columns):
    lines, chunks, tile, sub = columns // NLON, len(mids), NLON, 32
    total = columns + 2 * HALO * NLON

    def rows_of(width):
        return pl.BlockSpec((tile, width), lambda i, s: (i, 0))

    return pl.pallas_call(
        lambda *refs: col_kernel(lines, chunks, sub, *refs),
        out_shape=jax.ShapeDtypeStruct((rows, columns), jnp.float32),
        grid_spec=pltpu.PrefetchScalarGridSpec(
            num_scalar_prefetch=1,
            grid=(rows // tile,),
            in_specs=[rows_of(HALO * NLON)]
            + [rows_of(columns // chunks)] * chunks
            + [
                rows_of(HALO * NLON),
                pl.BlockSpec((5 * CYCLES, total), lambda i, s: (0, 0), pipeline_mode=pl.Buffered(1)),
                rows_of(6 * NLON),
            ],
            out_specs=rows_of(columns),
            scratch_shapes=[pltpu.VMEM((sub, total), jnp.float32)] * 3,
        ),
        compiler_params=pltpu.CompilerParams(vmem_limit_bytes=40 << 20),
        cost_estimate=pl.CostEstimate(
            flops=60 * rows * columns, transcendentals=0, bytes_accessed=12 * rows * columns
        ),
        name="col_sections",
    )(place, before, *mids, after, coef, noise)


def spread_noise(coef, noise, first, lines):
    around = lines + 4
    c = lines_of(coef, first - 6, lines + 12)[1]
    padded = jnp.pad(noise.reshape(-1, NLON), ((2 * HALO, 2 * HALO), (0, 0)))
    mine = lax.dynamic_slice_in_dim(padded, first - 2 + 2 * HALO, around, 0)
    eye = jnp.eye(NLON, dtype=jnp.float32)
    centre = mine[:, :, None] * eye[None]
    field = jnp.pad(centre[:, None], ((0, 0), (4, 4), (0, 0), (0, 0)))
    factors = jnp.stack([c[:, k:k + around] for k in range(9)], axis=2)[..., None]

    def step(g):
        mid = g[:, 1:-1]
        trim = (9 - mid.shape[1]) // 2
        f = factors[:, :, trim:9 - trim]
        return stencil(
            mid, jnp.roll(mid, -1, axis=2), jnp.roll(mid, 1, axis=2), g[:, 2:], g[:, :-2], f
        )

    first_step = step(field)
    both = 0.5 * (field[:, 2:-2] + step(first_step))
    pieces = [both[d:d + lines, 4 - d] for d in range(5)] + [centre[2:2 + lines]]
    return jnp.concatenate([p.reshape(lines * NLON, NLON) for p in pieces], axis=1)


def on_device(covariance, model_noise, east_wind, north_wind):
    rows, columns = covariance.shape
    row_lines, col_lines = rows // NLON, columns // NLON
    edge = HALO * NLON
    row_first = lax.axis_index("row") * row_lines
    col_first = lax.axis_index("col") * col_lines
    row_size, col_size = lax.axis_size("row"), lax.axis_size("col")
    row_up = [(i, i + 1) for i in range(row_size - 1)]
    row_down = [(j, i) for i, j in row_up]
    col_up = [(i, i + 1) for i in range(col_size - 1)]
    col_down = [(j, i) for i, j in col_up]

    chunks = columns // edge
    order = [0, chunks - 1] + list(range(1, chunks - 1))
    halos = {}
    for k in order:
        part = covariance[:, k * edge:(k + 1) * edge]
        halos[k] = (
            lax.ppermute(part[rows - edge:], "row", row_up),
            lax.ppermute(part[:edge], "row", row_down),
        )

    coef = coefficients(east_wind, north_wind)
    row_coef = lines_of(coef, row_first - HALO, row_lines + 2 * HALO).reshape(5 * CYCLES, -1)
    row_coef = jnp.broadcast_to(row_coef[:, :, None], row_coef.shape + (128,))
    col_coef = lines_of(coef, col_first - HALO, col_lines + 2 * HALO).reshape(5 * CYCLES, -1)
    noise = spread_noise(coef, model_noise, row_first, row_lines)

    mids = {}
    for k in order:
        mids[k] = row_sections(
            halos[k][0], covariance, halos[k][1], row_coef, rows, edge, k, min(256, edge)
        )
    after = lax.ppermute(mids[0], "col", col_down)
    before = lax.ppermute(mids[chunks - 1], "col", col_up)
    place = jnp.stack([row_first, col_first]).astype(jnp.int32)
    return col_sections(
        place, before, [mids[k] for k in range(chunks)], after, col_coef, noise, rows, columns
    )


def solution(mesh):
    in_specs = (P("row", "col"), P(), P(), P())
    out_specs = P("row", "col")
    return jax.shard_map(
        on_device, mesh=mesh, in_specs=in_specs, out_specs=out_specs, check_vma=False
    )
```

```python
import jax
import jax.numpy as jnp
from jax import lax
from jax.experimental import pallas as pl
from jax.experimental.pallas import tpu as pltpu
from jax.sharding import PartitionSpec as P

NLON = 128
CYCLES = 2
HALO = 2 * CYCLES


def coefficients(east, north):
    west = jnp.roll(east, 1, axis=-1)
    south = jnp.pad(north[:, :-1], ((0, 0), (1, 0), (0, 0)))
    up, down = (lambda v: jnp.maximum(v, 0.0)), (lambda v: jnp.minimum(v, 0.0))
    centre = 1.0 + ((down(west) - up(east)) + (down(south) - up(north)))
    to_north = -down(north)
    lines = north.shape[1]
    inside = (jnp.arange(lines) < lines - 1)[None, :, None]
    to_north = jnp.where(inside, to_north, 0.0)
    return jnp.stack([centre, -down(east), up(west), to_north, up(south)], axis=1)


def lines_of(coef, first, amount):
    padded = jnp.pad(coef, ((0, 0), (0, 0), (2 * HALO, 2 * HALO), (0, 0)))
    return lax.dynamic_slice_in_dim(padded, first + 2 * HALO, amount, 2)


def shifted(values, step):
    lines, lons = step
    if lines > 0:
        values = jnp.pad(values[lines:], ((0, lines), (0, 0)))
    elif lines < 0:
        values = jnp.pad(values[:lines], ((-lines, 0), (0, 0)))
    return jnp.roll(values, -lons, axis=1) if lons else values


REACH = [(-2, 0), (-1, -1), (-1, 0), (-1, 1), (0, -2), (0, -1), (0, 0), (0, 1), (0, 2), (1, -1), (1, 0), (1, 1), (2, 0)]


def spread_noise(coef, noise, scale):
    steps = [(0, 0), (0, 1), (0, -1), (1, 0), (-1, 0)]
    once = [coef[i] - 1.0 if i == 0 else coef[i] for i in range(5)]
    weights = {r: 0.0 for r in REACH}
    weights[(0, 0)] = 1.0
    for p, a in zip(steps, once):
        weights[p] = weights[p] + a
        for q, b in zip(steps, once):
            at = (p[0] + q[0], p[1] + q[1])
            weights[at] = weights[at] + 0.5 * a * shifted(b, p)
    noise = noise.reshape(-1, NLON)
    rows = [scale * weights[r] * shifted(noise, r) for r in REACH]
    zero = jnp.zeros_like(noise)
    return jnp.stack(rows + [noise, zero, zero], axis=1)


def stencil(centre, east, west, north, south, c):
    return (c[0] * centre + (c[1] * east + c[2] * west)) + (c[3] * north + c[4] * south)


LINE = NLON + 16
GROUPS = 4


def wrap(ref, lines, tiles):
    for l in lines:
        for t in range(tiles):
            ref[t, l * LINE:l * LINE + 8, :] = ref[t, l * LINE + NLON:l * LINE + NLON + 8, :]
            ref[t, l * LINE + NLON + 8:(l + 1) * LINE, :] = ref[t, l * LINE + 8:l * LINE + 16, :]


def stage(source, target, added, coef, cycle, first, last, tiles, write=None):
    def group(i, carry):
        at = pl.multiple_of(i * (8 * GROUPS), 8 * GROUPS)
        for k in range(0, 8 * GROUPS, 8):
            def read(t, l, o=0):
                return source[t, pl.ds(at + (l * LINE + 8 + k + o), 8), :]

            south = [read(t, first - 1) for t in range(tiles)]
            centre = [read(t, first) for t in range(tiles)]
            for l in range(first, last):
                c = [coef[cycle * 5 + n, pl.ds(at + (l * NLON + k), 8), :] for n in range(5)]
                for t in range(tiles):
                    north = read(t, l + 1)
                    value = stencil(centre[t], read(t, l, 1), read(t, l, -1), north, south[t], c)
                    if added is not None:
                        value = value + added[t, pl.ds(at + (l * LINE + 8 + k), 8), :]
                    if write is None:
                        target[t, pl.ds(at + (l * LINE + 8 + k), 8), :] = value
                    else:
                        write(t, l, at + k, value)
                    south[t], centre[t] = centre[t], north
        return carry

    lax.fori_loop(0, NLON // (8 * GROUPS), group, 0)
    if write is None:
        wrap(target, range(first, last), tiles)


def fill_factors(compact_ref, factors):
    rows = compact_ref.shape[0]

    def body(i, carry):
        at = pl.ds(pl.multiple_of(i * 32, 32), 32)
        block = compact_ref[at, :]
        for n in range(5 * CYCLES):
            factors[n, at, :] = jnp.broadcast_to(block[:, n:n + 1], (32, 128))
        return carry

    lax.fori_loop(0, rows // 32, body, 0)


def row_kernel(lines, before_ref, mid_ref, after_ref, compact_ref, out_ref, factors, field, one, two):
    total = lines + 2 * HALO
    tiles = field.shape[0]

    @pl.when(pl.program_id(0) == 0)
    def _():
        fill_factors(compact_ref, factors)

    def copy(ref, first, count):
        for l in range(count):
            for t in range(tiles):
                field[t, (first + l) * LINE + 8:(first + l) * LINE + 8 + NLON, :] = ref[
                    l * NLON:(l + 1) * NLON, t * 128:(t + 1) * 128
                ]

    copy(before_ref, 0, HALO)
    copy(mid_ref, HALO, lines)
    copy(after_ref, HALO + lines, HALO)
    wrap(field, range(total), tiles)

    def write(t, l, at, value):
        out_ref[pl.ds(at + (l - HALO) * NLON, 8), t * 128:(t + 1) * 128] = value

    stage(field, one, None, factors, 0, 1, total - 1, tiles)
    stage(one, two, field, factors, 0, 2, total - 2, tiles)
    stage(two, field, None, factors, 1, 3, total - 3, tiles)
    stage(field, None, two, factors, 1, 4, total - 4, tiles, write)


def row_sections(before, block, after, compact, rows, columns, start):
    tile = 256
    lines, per = rows // NLON, columns // tile
    total = lines + 2 * HALO
    return pl.pallas_call(
        lambda *refs: row_kernel(lines, *refs),
        out_shape=jax.ShapeDtypeStruct((rows, columns), jnp.float32),
        grid=(per,),
        in_specs=[
            pl.BlockSpec((HALO * NLON, tile), lambda i: (0, i)),
            pl.BlockSpec((rows, tile), lambda i: (0, start // tile + i)),
            pl.BlockSpec((HALO * NLON, tile), lambda i: (0, i)),
            pl.BlockSpec(compact.shape, lambda i: (0, 0), pipeline_mode=pl.Buffered(1)),
        ],
        out_specs=pl.BlockSpec((rows, tile), lambda i: (0, i)),
        scratch_shapes=[pltpu.VMEM((5 * CYCLES, total * NLON, 128), jnp.float32)]
        + [pltpu.VMEM((tile // 128, total * LINE, 128), jnp.float32)] * 3,
        compiler_params=pltpu.CompilerParams(vmem_limit_bytes=48 << 20),
        cost_estimate=pl.CostEstimate(
            flops=60 * rows * columns, transcendentals=0, bytes_accessed=12 * rows * columns
        ),
        name="row_sections",
    )(before, block, after, compact)


def col_kernel(lines, widths, place_ref, *refs):
    pieces = refs[:len(widths)]
    compact_ref, noise_ref, out_ref, factors, field, one, two = refs[len(widths):]
    total = lines + 2 * HALO
    tiles = field.shape[0]

    @pl.when(pl.program_id(0) == 0)
    def _():
        fill_factors(compact_ref, factors)

    l = 0
    for ref, width in zip(pieces, widths):
        for k in range(width // NLON):
            for t in range(tiles):
                field[t, l * LINE + 8:l * LINE + 8 + NLON, :] = ref[
                    t * 128:(t + 1) * 128, k * NLON:(k + 1) * NLON
                ].T
            l += 1
    wrap(field, range(total), tiles)

    row = lax.broadcasted_iota(jnp.int32, (NLON, NLON), 0)
    lane = lax.broadcasted_iota(jnp.int32, (NLON, NLON), 1)
    apart = (row - lane + NLON) % NLON

    stage(field, one, None, factors, 0, 1, total - 1, tiles)
    stage(one, two, field, factors, 0, 2, total - 2, tiles)
    for t in range(tiles):
        shift = place_ref[0] + pl.program_id(0) * tiles + t - place_ref[1]
        for d in range(-2, 3):
            at = shift + (d + HALO)

            @pl.when((at >= 2) & (at < total - 2))
            def _():
                value = jnp.zeros((NLON, NLON), jnp.float32)
                for n, (dl, di) in enumerate(REACH):
                    if dl == d:
                        band = jnp.broadcast_to(noise_ref[t, n:n + 1, :], (NLON, NLON))
                        value = jnp.where(apart == di % NLON, band, value)
                rows = pl.ds(pl.multiple_of(at * LINE + 8, 8), NLON)
                two[t, rows, :] = two[t, rows, :] + value
                low = pl.ds(pl.multiple_of(at * LINE, 8), 8)
                two[t, low, :] = two[t, low, :] + value[NLON - 8:]
                high = pl.ds(pl.multiple_of(at * LINE + NLON + 8, 8), 8)
                two[t, high, :] = two[t, high, :] + value[:8]

    stage(two, field, None, factors, 1, 3, total - 3, tiles)
    stage(field, one, two, factors, 1, 4, total - 4, tiles)
    for t in range(tiles):
        shift = place_ref[0] + pl.program_id(0) * tiles + t - place_ref[1]

        for l in range(HALO, total - HALO):
            out_ref[t * 128:(t + 1) * 128, (l - HALO) * NLON:(l - HALO + 1) * NLON] = (
                0.0625 * one[t, l * LINE + 8:l * LINE + 8 + NLON, :]
            ).T

        @pl.when((shift >= 0) & (shift < lines))
        def _():
            cols = pl.ds(pl.multiple_of(shift * NLON, NLON), NLON)
            band = jnp.broadcast_to(noise_ref[t, len(REACH):len(REACH) + 1, :], (NLON, NLON))
            here = out_ref[t * 128:(t + 1) * 128, cols]
            out_ref[t * 128:(t + 1) * 128, cols] = here + jnp.where(apart == 0, band, 0.0)


def col_sections(place, pieces, compact, noise, rows, columns):
    widths = [p.shape[1] for p in pieces]
    tile = 256
    tiles = tile // NLON
    lines = columns // NLON
    total = lines + 2 * HALO
    return pl.pallas_call(
        lambda *refs: col_kernel(lines, widths, *refs),
        out_shape=jax.ShapeDtypeStruct((rows, columns), jnp.float32),
        grid_spec=pltpu.PrefetchScalarGridSpec(
            num_scalar_prefetch=1,
            grid=(rows // tile,),
            in_specs=[pl.BlockSpec((tile, w), lambda i, s: (i, 0)) for w in widths]
            + [
                pl.BlockSpec(compact.shape, lambda i, s: (0, 0), pipeline_mode=pl.Buffered(1)),
                pl.BlockSpec((tiles, 16, NLON), lambda i, s: (i, 0, 0)),
            ],
            out_specs=pl.BlockSpec((tile, columns), lambda i, s: (i, 0)),
            scratch_shapes=[pltpu.VMEM((5 * CYCLES, total * NLON, 128), jnp.float32)]
            + [pltpu.VMEM((tiles, total * LINE, 128), jnp.float32)] * 3,
        ),
        compiler_params=pltpu.CompilerParams(vmem_limit_bytes=56 << 20),
        cost_estimate=pl.CostEstimate(
            flops=60 * rows * columns, transcendentals=0, bytes_accessed=12 * rows * columns
        ),
        name="col_sections",
    )(place, *pieces, compact, noise)


def on_device(covariance, model_noise, east_wind, north_wind):
    rows, columns = covariance.shape
    row_lines, col_lines = rows // NLON, columns // NLON
    edge = HALO * NLON
    row_first = lax.axis_index("row") * row_lines
    col_first = lax.axis_index("col") * col_lines
    row_size, col_size = lax.axis_size("row"), lax.axis_size("col")
    row_up = [(i, i + 1) for i in range(row_size - 1)]
    row_down = [(j, i) for i, j in row_up]
    col_up = [(i, i + 1) for i in range(col_size - 1)]
    col_down = [(j, i) for i, j in col_up]

    half = edge // 2
    far = columns - edge
    order = [(0, half), (far, half), (half, half), (far + half, half)]
    order += [(c, edge) for c in range(edge, far, edge)]
    halos = {}
    for start, width in order:
        halos[start] = (
            lax.ppermute(covariance[rows - edge:, start:start + width], "row", row_up),
            lax.ppermute(covariance[:edge, start:start + width], "row", row_down),
        )

    coef = coefficients(east_wind, north_wind)

    def compact(first, lines):
        c = lines_of(coef, first, lines).reshape(5 * CYCLES, -1).T
        return jnp.pad(c, ((0, 0), (0, 16 - 5 * CYCLES)))

    row_coef = compact(row_first - HALO, row_lines + 2 * HALO)
    col_coef = compact(col_first - HALO, col_lines + 2 * HALO)
    noise = lax.dynamic_slice_in_dim(
        spread_noise(coef[1], model_noise, 8.0), row_first, row_lines, 0
    )

    mids, before, after = {}, [], []
    for start, width in order:
        mids[start] = row_sections(
            halos[start][0], covariance, halos[start][1], row_coef, rows, width, start
        )
        if start < edge:
            after.append(lax.ppermute(mids[start], "col", col_down))
        elif start >= far:
            before.append(lax.ppermute(mids[start], "col", col_up))
    place = jnp.stack([row_first, col_first]).astype(jnp.int32)
    pieces = before + [mids[start] for start in sorted(mids)] + after
    return col_sections(place, pieces, col_coef, noise, rows, columns)


def solution(mesh):
    in_specs = (P("row", "col"), P(), P(), P())
    out_specs = P("row", "col")
    return jax.shard_map(
        on_device, mesh=mesh, in_specs=in_specs, out_specs=out_specs, check_vma=False
    )
```

```python
import jax
import jax.numpy as jnp
from jax import lax
from jax.experimental import pallas as pl
from jax.experimental.pallas import tpu as pltpu
from jax.sharding import PartitionSpec as P

NLON = 128
CYCLES = 2
HALO = 2 * CYCLES


def coefficients(east, north):
    west = jnp.roll(east, 1, axis=-1)
    south = jnp.pad(north[:, :-1], ((0, 0), (1, 0), (0, 0)))
    up, down = (lambda v: jnp.maximum(v, 0.0)), (lambda v: jnp.minimum(v, 0.0))
    centre = 1.0 + ((down(west) - up(east)) + (down(south) - up(north)))
    to_north = -down(north)
    lines = north.shape[1]
    inside = (jnp.arange(lines) < lines - 1)[None, :, None]
    to_north = jnp.where(inside, to_north, 0.0)
    return jnp.stack([centre, -down(east), up(west), to_north, up(south)], axis=1)


def lines_of(coef, first, amount):
    padded = jnp.pad(coef, ((0, 0), (0, 0), (2 * HALO, 2 * HALO), (0, 0)))
    return lax.dynamic_slice_in_dim(padded, first + 2 * HALO, amount, 2)


def shifted(values, step):
    lines, lons = step
    if lines > 0:
        values = jnp.pad(values[lines:], ((0, lines), (0, 0)))
    elif lines < 0:
        values = jnp.pad(values[:lines], ((-lines, 0), (0, 0)))
    return jnp.roll(values, -lons, axis=1) if lons else values


REACH = [(-2, 0), (-1, -1), (-1, 0), (-1, 1), (0, -2), (0, -1), (0, 0), (0, 1), (0, 2), (1, -1), (1, 0), (1, 1), (2, 0)]


def spread_noise(coef, noise, scale):
    steps = [(0, 0), (0, 1), (0, -1), (1, 0), (-1, 0)]
    once = [coef[i] - 1.0 if i == 0 else coef[i] for i in range(5)]
    weights = {r: 0.0 for r in REACH}
    weights[(0, 0)] = 1.0
    for p, a in zip(steps, once):
        weights[p] = weights[p] + a
        for q, b in zip(steps, once):
            at = (p[0] + q[0], p[1] + q[1])
            weights[at] = weights[at] + 0.5 * a * shifted(b, p)
    noise = noise.reshape(-1, NLON)
    rows = [scale * weights[r] * shifted(noise, r) for r in REACH]
    zero = jnp.zeros_like(noise)
    return jnp.stack(rows + [noise, zero, zero], axis=1)


def stencil(centre, east, west, north, south, c):
    return (c[0] * centre + (c[1] * east + c[2] * west)) + (c[3] * north + c[4] * south)


LINE = NLON + 16
GROUPS = 4


def wrap(ref, lines, tiles):
    for l in lines:
        for t in range(tiles):
            ref[t, l * LINE:l * LINE + 8, :] = ref[t, l * LINE + NLON:l * LINE + NLON + 8, :]
            ref[t, l * LINE + NLON + 8:(l + 1) * LINE, :] = ref[t, l * LINE + 8:l * LINE + 16, :]


def stage(source, target, added, coef, cycle, first, last, tiles, write=None):
    def group(i, carry):
        at = pl.multiple_of(i * (8 * GROUPS), 8 * GROUPS)
        for k in range(0, 8 * GROUPS, 8):
            def read(t, l, o=0):
                return source[t, pl.ds(at + (l * LINE + 8 + k + o), 8), :]

            south = [read(t, first - 1) for t in range(tiles)]
            centre = [read(t, first) for t in range(tiles)]
            for l in range(first, last):
                c = [coef[cycle * 5 + n, pl.ds(at + (l * NLON + k), 8), :] for n in range(5)]
                for t in range(tiles):
                    north = read(t, l + 1)
                    value = stencil(centre[t], read(t, l, 1), read(t, l, -1), north, south[t], c)
                    if added is not None:
                        value = value + added[t, pl.ds(at + (l * LINE + 8 + k), 8), :]
                    if write is None:
                        target[t, pl.ds(at + (l * LINE + 8 + k), 8), :] = value
                    else:
                        write(t, l, at + k, value)
                    south[t], centre[t] = centre[t], north
        return carry

    lax.fori_loop(0, NLON // (8 * GROUPS), group, 0)
    if write is None:
        wrap(target, range(first, last), tiles)


def fill_factors(compact_ref, factors):
    rows = compact_ref.shape[0]

    def body(i, carry):
        at = pl.ds(pl.multiple_of(i * 32, 32), 32)
        block = compact_ref[at, :]
        for n in range(5 * CYCLES):
            factors[n, at, :] = jnp.broadcast_to(block[:, n:n + 1], (32, 128))
        return carry

    lax.fori_loop(0, rows // 32, body, 0)


def row_kernel(lines, before_ref, mid_ref, after_ref, factors, out_ref, field, one, two):
    total = lines + 2 * HALO
    tiles = field.shape[0]

    def copy(ref, first, count):
        for l in range(count):
            for t in range(tiles):
                field[t, (first + l) * LINE + 8:(first + l) * LINE + 8 + NLON, :] = ref[
                    l * NLON:(l + 1) * NLON, t * 128:(t + 1) * 128
                ]

    copy(before_ref, 0, HALO)
    copy(mid_ref, HALO, lines)
    copy(after_ref, HALO + lines, HALO)
    wrap(field, range(total), tiles)

    def write(t, l, at, value):
        out_ref[pl.ds(at + (l - HALO) * NLON, 8), t * 128:(t + 1) * 128] = value

    stage(field, one, None, factors, 0, 1, total - 1, tiles)
    stage(one, two, field, factors, 0, 2, total - 2, tiles)
    stage(two, field, None, factors, 1, 3, total - 3, tiles)
    stage(field, None, two, factors, 1, 4, total - 4, tiles, write)


def row_sections(before, block, after, factors, rows, columns, start):
    tile = 256
    lines, per = rows // NLON, columns // tile
    total = lines + 2 * HALO
    return pl.pallas_call(
        lambda *refs: row_kernel(lines, *refs),
        out_shape=jax.ShapeDtypeStruct((rows, columns), jnp.float32),
        grid=(per,),
        in_specs=[
            pl.BlockSpec((HALO * NLON, tile), lambda i: (0, i)),
            pl.BlockSpec((rows, tile), lambda i: (0, start // tile + i)),
            pl.BlockSpec((HALO * NLON, tile), lambda i: (0, i)),
            pl.BlockSpec(factors.shape, lambda i: (0, 0, 0), pipeline_mode=pl.Buffered(1)),
        ],
        out_specs=pl.BlockSpec((rows, tile), lambda i: (0, i)),
        scratch_shapes=[pltpu.VMEM((tile // 128, total * LINE, 128), jnp.float32)] * 3,
        compiler_params=pltpu.CompilerParams(vmem_limit_bytes=48 << 20),
        cost_estimate=pl.CostEstimate(
            flops=60 * rows * columns, transcendentals=0, bytes_accessed=12 * rows * columns
        ),
        name="row_sections",
    )(before, block, after, factors)


def col_kernel(lines, widths, place_ref, *refs):
    pieces = refs[:len(widths)]
    compact_ref, noise_ref, out_ref, factors, field, one, two = refs[len(widths):]
    total = lines + 2 * HALO
    tiles = field.shape[0]

    @pl.when(pl.program_id(0) == 0)
    def _():
        fill_factors(compact_ref, factors)

    l = 0
    for ref, width in zip(pieces, widths):
        for k in range(width // NLON):
            for t in range(tiles):
                field[t, l * LINE + 8:l * LINE + 8 + NLON, :] = ref[
                    t * 128:(t + 1) * 128, k * NLON:(k + 1) * NLON
                ].T
            l += 1
    wrap(field, range(total), tiles)

    row = lax.broadcasted_iota(jnp.int32, (NLON, NLON), 0)
    lane = lax.broadcasted_iota(jnp.int32, (NLON, NLON), 1)
    apart = (row - lane + NLON) % NLON

    stage(field, one, None, factors, 0, 1, total - 1, tiles)
    stage(one, two, field, factors, 0, 2, total - 2, tiles)
    for t in range(tiles):
        shift = place_ref[0] + pl.program_id(0) * tiles + t - place_ref[1]
        for d in range(-2, 3):
            at = shift + (d + HALO)

            @pl.when((at >= 2) & (at < total - 2))
            def _():
                value = jnp.zeros((NLON, NLON), jnp.float32)
                for n, (dl, di) in enumerate(REACH):
                    if dl == d:
                        band = jnp.broadcast_to(noise_ref[t, n:n + 1, :], (NLON, NLON))
                        value = jnp.where(apart == di % NLON, band, value)
                rows = pl.ds(pl.multiple_of(at * LINE + 8, 8), NLON)
                two[t, rows, :] = two[t, rows, :] + value
                low = pl.ds(pl.multiple_of(at * LINE, 8), 8)
                two[t, low, :] = two[t, low, :] + value[NLON - 8:]
                high = pl.ds(pl.multiple_of(at * LINE + NLON + 8, 8), 8)
                two[t, high, :] = two[t, high, :] + value[:8]

    stage(two, field, None, factors, 1, 3, total - 3, tiles)
    stage(field, one, two, factors, 1, 4, total - 4, tiles)
    for t in range(tiles):
        shift = place_ref[0] + pl.program_id(0) * tiles + t - place_ref[1]

        for l in range(HALO, total - HALO):
            out_ref[t * 128:(t + 1) * 128, (l - HALO) * NLON:(l - HALO + 1) * NLON] = (
                0.0625 * one[t, l * LINE + 8:l * LINE + 8 + NLON, :]
            ).T

        @pl.when((shift >= 0) & (shift < lines))
        def _():
            cols = pl.ds(pl.multiple_of(shift * NLON, NLON), NLON)
            band = jnp.broadcast_to(noise_ref[t, len(REACH):len(REACH) + 1, :], (NLON, NLON))
            here = out_ref[t * 128:(t + 1) * 128, cols]
            out_ref[t * 128:(t + 1) * 128, cols] = here + jnp.where(apart == 0, band, 0.0)


def col_sections(place, pieces, compact, noise, rows, columns):
    widths = [p.shape[1] for p in pieces]
    tile = 256
    tiles = tile // NLON
    lines = columns // NLON
    total = lines + 2 * HALO
    return pl.pallas_call(
        lambda *refs: col_kernel(lines, widths, *refs),
        out_shape=jax.ShapeDtypeStruct((rows, columns), jnp.float32),
        grid_spec=pltpu.PrefetchScalarGridSpec(
            num_scalar_prefetch=1,
            grid=(rows // tile,),
            in_specs=[pl.BlockSpec((tile, w), lambda i, s: (i, 0)) for w in widths]
            + [
                pl.BlockSpec(compact.shape, lambda i, s: (0, 0), pipeline_mode=pl.Buffered(1)),
                pl.BlockSpec((tiles, 16, NLON), lambda i, s: (i, 0, 0)),
            ],
            out_specs=pl.BlockSpec((tile, columns), lambda i, s: (i, 0)),
            scratch_shapes=[pltpu.VMEM((5 * CYCLES, total * NLON, 128), jnp.float32)]
            + [pltpu.VMEM((tiles, total * LINE, 128), jnp.float32)] * 3,
        ),
        compiler_params=pltpu.CompilerParams(vmem_limit_bytes=56 << 20),
        cost_estimate=pl.CostEstimate(
            flops=60 * rows * columns, transcendentals=0, bytes_accessed=12 * rows * columns
        ),
        name="col_sections",
    )(place, *pieces, compact, noise)


def on_device(covariance, model_noise, east_wind, north_wind):
    rows, columns = covariance.shape
    row_lines, col_lines = rows // NLON, columns // NLON
    edge = HALO * NLON
    row_first = lax.axis_index("row") * row_lines
    col_first = lax.axis_index("col") * col_lines
    row_size, col_size = lax.axis_size("row"), lax.axis_size("col")
    row_up = [(i, i + 1) for i in range(row_size - 1)]
    row_down = [(j, i) for i, j in row_up]
    col_up = [(i, i + 1) for i in range(col_size - 1)]
    col_down = [(j, i) for i, j in col_up]

    far = columns - edge
    order = [(0, edge), (far, edge)] + ([(edge, far - edge)] if far > edge else [])
    halos = {}
    for start, width in order:
        halos[start] = (
            lax.ppermute(covariance[rows - edge:, start:start + width], "row", row_up),
            lax.ppermute(covariance[:edge, start:start + width], "row", row_down),
        )

    coef = coefficients(east_wind, north_wind)

    def compact(first, lines):
        c = lines_of(coef, first, lines).reshape(5 * CYCLES, -1).T
        return jnp.pad(c, ((0, 0), (0, 16 - 5 * CYCLES)))

    row_coef = lines_of(coef, row_first - HALO, row_lines + 2 * HALO).reshape(5 * CYCLES, -1)
    row_coef = jnp.broadcast_to(row_coef[:, :, None], row_coef.shape + (128,))
    col_coef = compact(col_first - HALO, col_lines + 2 * HALO)
    noise = lax.dynamic_slice_in_dim(
        spread_noise(coef[1], model_noise, 8.0), row_first, row_lines, 0
    )

    mids, before, after = {}, [], []
    for start, width in order:
        mids[start] = row_sections(
            halos[start][0], covariance, halos[start][1], row_coef, rows, width, start
        )
        if start < edge:
            after.append(lax.ppermute(mids[start], "col", col_down))
        elif start >= far:
            before.append(lax.ppermute(mids[start], "col", col_up))
    place = jnp.stack([row_first, col_first]).astype(jnp.int32)
    pieces = before + [mids[start] for start in sorted(mids)] + after
    return col_sections(place, pieces, col_coef, noise, rows, columns)


def solution(mesh):
    in_specs = (P("row", "col"), P(), P(), P())
    out_specs = P("row", "col")
    return jax.shard_map(
        on_device, mesh=mesh, in_specs=in_specs, out_specs=out_specs, check_vma=False
    )
```

```python
import jax
import jax.numpy as jnp
from jax import lax
from jax.experimental import pallas as pl
from jax.experimental.pallas import tpu as pltpu
from jax.sharding import PartitionSpec as P

NLON = 128
CYCLES = 2
HALO = 2 * CYCLES


def coefficients(east, north):
    west = jnp.roll(east, 1, axis=-1)
    south = jnp.pad(north[:, :-1], ((0, 0), (1, 0), (0, 0)))
    up, down = (lambda v: jnp.maximum(v, 0.0)), (lambda v: jnp.minimum(v, 0.0))
    centre = 1.0 + ((down(west) - up(east)) + (down(south) - up(north)))
    to_north = -down(north)
    lines = north.shape[1]
    inside = (jnp.arange(lines) < lines - 1)[None, :, None]
    to_north = jnp.where(inside, to_north, 0.0)
    return jnp.stack([centre, -down(east), up(west), to_north, up(south)], axis=1)


def lines_of(coef, first, amount):
    padded = jnp.pad(coef, ((0, 0), (0, 0), (2 * HALO, 2 * HALO), (0, 0)))
    return lax.dynamic_slice_in_dim(padded, first + 2 * HALO, amount, 2)


def shifted(values, step):
    lines, lons = step
    if lines > 0:
        values = jnp.pad(values[lines:], ((0, lines), (0, 0)))
    elif lines < 0:
        values = jnp.pad(values[:lines], ((-lines, 0), (0, 0)))
    return jnp.roll(values, -lons, axis=1) if lons else values


REACH = [(-2, 0), (-1, -1), (-1, 0), (-1, 1), (0, -2), (0, -1), (0, 0), (0, 1), (0, 2), (1, -1), (1, 0), (1, 1), (2, 0)]


def spread_noise(coef, noise, scale):
    steps = [(0, 0), (0, 1), (0, -1), (1, 0), (-1, 0)]
    once = [coef[i] - 1.0 if i == 0 else coef[i] for i in range(5)]
    weights = {r: 0.0 for r in REACH}
    weights[(0, 0)] = 1.0
    for p, a in zip(steps, once):
        weights[p] = weights[p] + a
        for q, b in zip(steps, once):
            at = (p[0] + q[0], p[1] + q[1])
            weights[at] = weights[at] + 0.5 * a * shifted(b, p)
    noise = noise.reshape(-1, NLON)
    rows = [scale * weights[r] * shifted(noise, r) for r in REACH]
    zero = jnp.zeros_like(noise)
    return jnp.stack(rows + [noise, zero, zero], axis=1)


def stencil(centre, east, west, north, south, c):
    return (c[0] * centre + (c[1] * east + c[2] * west)) + (c[3] * north + c[4] * south)


LINE = NLON + 16
GROUPS = 4


def wrap(ref, lines, tiles):
    for l in lines:
        for t in range(tiles):
            ref[t, l * LINE:l * LINE + 8, :] = ref[t, l * LINE + NLON:l * LINE + NLON + 8, :]
            ref[t, l * LINE + NLON + 8:(l + 1) * LINE, :] = ref[t, l * LINE + 8:l * LINE + 16, :]


def stage(source, target, added, coef, cycle, first, last, tiles, write=None):
    def group(i, carry):
        at = pl.multiple_of(i * (8 * GROUPS), 8 * GROUPS)
        for k in range(0, 8 * GROUPS, 8):
            def read(t, l, o=0):
                return source[t, pl.ds(at + (l * LINE + 8 + k + o), 8), :]

            south = [read(t, first - 1) for t in range(tiles)]
            centre = [read(t, first) for t in range(tiles)]
            for l in range(first, last):
                c = [coef[cycle * 5 + n, pl.ds(at + (l * NLON + k), 8), :] for n in range(5)]
                for t in range(tiles):
                    north = read(t, l + 1)
                    value = stencil(centre[t], read(t, l, 1), read(t, l, -1), north, south[t], c)
                    if added is not None:
                        value = value + added[t, pl.ds(at + (l * LINE + 8 + k), 8), :]
                    if write is None:
                        target[t, pl.ds(at + (l * LINE + 8 + k), 8), :] = value
                    else:
                        write(t, l, at + k, value)
                    south[t], centre[t] = centre[t], north
        return carry

    lax.fori_loop(0, NLON // (8 * GROUPS), group, 0)
    if write is None:
        wrap(target, range(first, last), tiles)


def row_kernel(lines, before_ref, mid_ref, after_ref, factors, out_ref, field, one, two):
    total = lines + 2 * HALO
    tiles = field.shape[0]

    def copy(ref, first, count):
        for l in range(count):
            for t in range(tiles):
                field[t, (first + l) * LINE + 8:(first + l) * LINE + 8 + NLON, :] = ref[
                    l * NLON:(l + 1) * NLON, t * 128:(t + 1) * 128
                ]

    copy(before_ref, 0, HALO)
    copy(mid_ref, HALO, lines)
    copy(after_ref, HALO + lines, HALO)
    wrap(field, range(total), tiles)

    def write(t, l, at, value):
        out_ref[pl.ds(at + (l - HALO) * NLON, 8), t * 128:(t + 1) * 128] = value

    stage(field, one, None, factors, 0, 1, total - 1, tiles)
    stage(one, two, field, factors, 0, 2, total - 2, tiles)
    stage(two, field, None, factors, 1, 3, total - 3, tiles)
    stage(field, None, two, factors, 1, 4, total - 4, tiles, write)


def row_sections(before, block, after, factors, rows, columns, start):
    tile = 256
    lines, per = rows // NLON, columns // tile
    total = lines + 2 * HALO
    return pl.pallas_call(
        lambda *refs: row_kernel(lines, *refs),
        out_shape=jax.ShapeDtypeStruct((rows, columns), jnp.float32),
        grid=(per,),
        in_specs=[
            pl.BlockSpec((HALO * NLON, tile), lambda i: (0, i)),
            pl.BlockSpec((rows, tile), lambda i: (0, start // tile + i)),
            pl.BlockSpec((HALO * NLON, tile), lambda i: (0, i)),
            pl.BlockSpec(factors.shape, lambda i: (0, 0, 0), pipeline_mode=pl.Buffered(1)),
        ],
        out_specs=pl.BlockSpec((rows, tile), lambda i: (0, i)),
        scratch_shapes=[pltpu.VMEM((tile // 128, total * LINE, 128), jnp.float32)] * 3,
        compiler_params=pltpu.CompilerParams(vmem_limit_bytes=48 << 20),
        cost_estimate=pl.CostEstimate(
            flops=60 * rows * columns, transcendentals=0, bytes_accessed=12 * rows * columns
        ),
        name="row_sections",
    )(before, block, after, factors)


def col_kernel(lines, widths, sub, place_ref, *refs):
    coef_ref, noise_ref, out_ref, one, two, three = refs[len(widths):]
    total = lines + 2 * HALO
    held = [(ref, k) for ref, width in zip(refs, widths) for k in range(width // NLON)]
    row_line = place_ref[0] + pl.program_id(0) * out_ref.shape[0] // NLON
    shift = row_line - place_ref[1]

    def lane(l):
        return slice(l * NLON, (l + 1) * NLON)

    def part(j, carry):
        rows = pl.ds(pl.multiple_of(j * sub, sub), sub)

        def source(l):
            ref, k = held[l]
            return ref[rows, lane(k)]

        def kept(ref):
            return lambda l: ref[:, lane(l)]

        def step(read, l, cycle):
            c = [
                jnp.broadcast_to(coef_ref[cycle * 5 + i:cycle * 5 + i + 1, lane(l)], (sub, NLON))
                for i in range(5)
            ]
            g = read(l)
            return stencil(
                g, pltpu.roll(g, NLON - 1, 1), pltpu.roll(g, 1, 1), read(l + 1), read(l - 1), c
            )

        for l in range(1, total - 1):
            one[:, lane(l)] = step(source, l, 0)
        for l in range(2, total - 2):
            two[:, lane(l)] = 0.5 * (source(l) + step(kept(one), l, 0))
        for d in range(5):
            at = shift + (d - 2 + HALO)

            @pl.when((at >= 2) & (at < total - 2))
            def _():
                cols = pl.ds(pl.multiple_of(at * NLON, NLON), NLON)
                two[:, cols] = two[:, cols] + noise_ref[rows, lane(d)]

        for l in range(3, total - 3):
            three[:, lane(l)] = step(kept(two), l, 1)
        for l in range(4, total - 4):
            out_ref[rows, lane(l - HALO)] = 0.125 * (kept(two)(l) + step(kept(three), l, 1))

        @pl.when((shift >= 0) & (shift < lines))
        def _():
            cols = pl.ds(pl.multiple_of(shift * NLON, NLON), NLON)
            out_ref[rows, cols] = out_ref[rows, cols] + noise_ref[rows, lane(5)]

        return carry

    lax.fori_loop(0, out_ref.shape[0] // sub, part, 0)


def col_sections(place, pieces, coef, noise, rows, columns):
    lines, tile, sub = columns // NLON, NLON, 32
    widths = [p.shape[1] for p in pieces]
    total = columns + 2 * HALO * NLON

    def rows_of(width):
        return pl.BlockSpec((tile, width), lambda i, s: (i, 0))

    return pl.pallas_call(
        lambda *refs: col_kernel(lines, widths, sub, *refs),
        out_shape=jax.ShapeDtypeStruct((rows, columns), jnp.float32),
        grid_spec=pltpu.PrefetchScalarGridSpec(
            num_scalar_prefetch=1,
            grid=(rows // tile,),
            in_specs=[rows_of(w) for w in widths]
            + [
                pl.BlockSpec((5 * CYCLES, total), lambda i, s: (0, 0), pipeline_mode=pl.Buffered(1)),
                rows_of(6 * NLON),
            ],
            out_specs=rows_of(columns),
            scratch_shapes=[pltpu.VMEM((sub, total), jnp.float32)] * 3,
        ),
        compiler_params=pltpu.CompilerParams(vmem_limit_bytes=40 << 20),
        cost_estimate=pl.CostEstimate(
            flops=60 * rows * columns, transcendentals=0, bytes_accessed=12 * rows * columns
        ),
        name="col_sections",
    )(place, *pieces, coef, noise)


def noise_cells(bands):
    lon = jnp.arange(NLON, dtype=jnp.int32)
    apart = (lon[None, :] - lon[:, None]) % NLON
    cells = []
    for d in range(-2, 3):
        cell = 0.0
        for n, (dl, di) in enumerate(REACH):
            if dl == d:
                cell = jnp.where(apart == di % NLON, bands[:, n, :, None], cell)
        cells.append(cell)
    cells.append(jnp.where(apart == 0, bands[:, len(REACH), :, None], 0.0))
    return jnp.concatenate([c.reshape(-1, NLON) for c in cells], axis=1)


def on_device(covariance, model_noise, east_wind, north_wind):
    rows, columns = covariance.shape
    row_lines, col_lines = rows // NLON, columns // NLON
    edge = HALO * NLON
    row_first = lax.axis_index("row") * row_lines
    col_first = lax.axis_index("col") * col_lines
    row_size, col_size = lax.axis_size("row"), lax.axis_size("col")
    row_up = [(i, i + 1) for i in range(row_size - 1)]
    row_down = [(j, i) for i, j in row_up]
    col_up = [(i, i + 1) for i in range(col_size - 1)]
    col_down = [(j, i) for i, j in col_up]

    far = columns - edge
    order = [(0, edge), (far, edge)] + ([(edge, far - edge)] if far > edge else [])
    halos = {}
    for start, width in order:
        halos[start] = (
            lax.ppermute(covariance[rows - edge:, start:start + width], "row", row_up),
            lax.ppermute(covariance[:edge, start:start + width], "row", row_down),
        )

    coef = coefficients(east_wind, north_wind)

    row_coef = lines_of(coef, row_first - HALO, row_lines + 2 * HALO).reshape(5 * CYCLES, -1)
    row_coef = jnp.broadcast_to(row_coef[:, :, None], row_coef.shape + (128,))
    col_coef = lines_of(coef, col_first - HALO, col_lines + 2 * HALO).reshape(5 * CYCLES, -1)
    noise = lax.dynamic_slice_in_dim(
        spread_noise(coef[1], model_noise, 4.0), row_first, row_lines, 0
    )

    mids, before, after = {}, [], []
    for start, width in order:
        mids[start] = row_sections(
            halos[start][0], covariance, halos[start][1], row_coef, rows, width, start
        )
        if start < edge:
            after.append(lax.ppermute(mids[start], "col", col_down))
        elif start >= far:
            before.append(lax.ppermute(mids[start], "col", col_up))
    place = jnp.stack([row_first, col_first]).astype(jnp.int32)
    pieces = before + [mids[start] for start in sorted(mids)] + after
    return col_sections(place, pieces, col_coef, noise_cells(noise), rows, columns)


def solution(mesh):
    in_specs = (P("row", "col"), P(), P(), P())
    out_specs = P("row", "col")
    return jax.shard_map(
        on_device, mesh=mesh, in_specs=in_specs, out_specs=out_specs, check_vma=False
    )
```
